32 devices in a mesh: dp: 8 (over y, x, core), seq: 4 (over z).
Axes of the slice: x: 2, y: 2, z: 4, core: 2. Of those that a mesh axis runs over, the one named last changes fastest.
Arguments:
- inputs: bfloat16 [32, 512, 1024], P('dp', 'seq'), may hold values from -6 to 6
- cotangent: bfloat16 [32, 512, 1024], P('dp', 'seq'), may hold values from -6 to 6
- lengths: int32 [32], P('dp'), may hold values from 80 to 512, as said below
- w_query: bfloat16 [1024, 1024], replicated, may hold values from -0.1875 to 0.1875
- b_query: float32 [1024], replicated, may hold values from -4 to 4
- w_key: bfloat16 [1024, 1024], replicated, may hold values from -0.1875 to 0.1875
- w_value: bfloat16 [1024, 1024], replicated, may hold values from -0.1875 to 0.1875
- b_value: float32 [1024], replicated, may hold values from -4 to 4
- w_output: bfloat16 [1024, 1024], replicated, may hold values from -0.75 to 0.75
- b_output: float32 [1024], replicated, may hold values from -4 to 4
- gain_first: float32 [1024], replicated, may hold values from 0.5 to 1.5
- shift_first: float32 [1024], replicated, may hold values from -4 to 4
- w_in: bfloat16 [1024, 4096], replicated, may hold values from -0.1875 to 0.1875
- b_in: float32 [4096], replicated, may hold values from -4 to 4
- w_out: bfloat16 [4096, 1024], replicated, may hold values from -0.1875 to 0.1875
- b_out: float32 [1024], replicated, may hold values from -4 to 4
- gain_second: float32 [1024], replicated, may hold values from 0.5 to 1.5
- shift_second: float32 [1024], replicated, may hold values from -4 to 4
Outputs:
- outputs: bfloat16 [32, 512, 1024], P('dp', 'seq')
- grad_inputs: float32 [32, 512, 1024], P('dp', 'seq')
- grad_w_query: float32 [1024, 1024], P(('dp', 'seq'))
- grad_b_query: float32 [1024], P(('dp', 'seq'))
- grad_w_key: float32 [1024, 1024], P(('dp', 'seq'))
- grad_w_value: float32 [1024, 1024], P(('dp', 'seq'))
- grad_b_value: float32 [1024], P(('dp', 'seq'))
- grad_w_output: float32 [1024, 1024], P(('dp', 'seq'))
- grad_b_output: float32 [1024], P(('dp', 'seq'))
- grad_gain_first: float32 [1024], P(('dp', 'seq'))
- grad_shift_first: float32 [1024], P(('dp', 'seq'))
- grad_w_in: float32 [1024, 4096], P(('dp', 'seq'))
- grad_b_in: float32 [4096], P(('dp', 'seq'))
- grad_w_out: float32 [4096, 1024], P(('dp', 'seq'))
- grad_b_out: float32 [1024], P(('dp', 'seq'))
- grad_gain_second: float32 [1024], P(('dp', 'seq'))
- grad_shift_second: float32 [1024], P(('dp', 'seq'))
The draws below stay inside these ranges and needn't reach their ends.
Inputs may be any that keep to these rules, and one draw needn't show every extreme that they name: A page's real tokens are its first lengths slots. Some page is full and some page has exactly 80 real tokens.
All inputs are finite; a program needn't handle non-finite values.
Results may differ from the reference program's by a relative error of at most 0.015.
Values may be sent and summed in bfloat16 or wider, within the bound.
No kernel may reach another device: no remote copies, remote signals or barrier semaphores. Data moves between devices by JAX's collectives and lax.ppermute only.
A program may use at most 320 MiB of HBM per device.

```python
import jax
import jax.numpy as jnp
from jax import lax

D = 1024
HEADS = 16
HEAD_DIM = 64
FF = 4096
SLOTS = 512
MIN_LEN = 80
P_DEV = 4
PAGES = 32


def draw_lengths(key, part):
    streams = jax.random.split(key, 3)
    base = jax.random.randint(streams[0], (PAGES,), MIN_LEN, SLOTS + 1)
    full_at = jax.random.randint(streams[1], (), 0, PAGES)
    short_at = (full_at + jax.random.randint(streams[2], (), 1, PAGES)) % PAGES
    places = jnp.arange(PAGES)
    chosen = jnp.where(places == full_at, SLOTS, jnp.where(places == short_at, MIN_LEN, base))
    return chosen.astype(jnp.int32)


def spiked(values, stream_key, source, target, parts, factor):
    def block_of(axis_at):
        return (jnp.arange(values.shape[axis_at]) // (values.shape[axis_at] // parts)).reshape((-1,) + (1,) * (values.ndim - 1 - axis_at))

    one_side = jax.random.permutation(stream_key, parts)[block_of(target)]
    second = (block_of(target) + parts // 2) % parts
    return jnp.where((block_of(source) == one_side) | (block_of(source) == second), factor * values, values)


def steps_of(own_key, shape, cuts, least, top_value):
    def one(axis_at, shards_of):
        heights = jax.random.uniform(jax.random.fold_in(jax.random.fold_in(own_key, 6), axis_at), (shards_of,), jnp.float32, least / len(cuts), top_value / len(cuts))
        return jnp.repeat(jnp.exp(heights), shape[axis_at] // shards_of).reshape((-1,) + (1,) * (len(shape) - axis_at - 1))

    level = one(*cuts[0])
    for cut in cuts[1:]:
        level = level * one(*cut)
    return level


def scatter_about(stream_key, extent, spread, bound, cuts=(), dtype=jnp.bfloat16):
    array = spread * jax.random.normal(stream_key, extent, jnp.float32)
    if cuts:
        array = array * steps_of(stream_key, extent, cuts, -0.22, 0.18)
    return jnp.clip(array, -bound, bound).astype(dtype)


def gaussian_with(key, dims, scale, bound, cuts, heavy, dtype=jnp.bfloat16):
    values = scale * jax.random.normal(key, dims, jnp.float32)
    if cuts:
        values = values * steps_of(key, dims, cuts, -0.22, 0.18)
    return jnp.clip(spiked(values, jax.random.fold_in(key, 3), *heavy), -bound, bound).astype(dtype)


def setup_inputs(seed: int = 0) -> dict:
    arg_keys = jax.random.split(jax.random.key(seed), 19)
    return {
        "inputs": gaussian_with(arg_keys[0], (PAGES, SLOTS, D), 1.0, 6.0, ((0, 8), (1, 4)), (0, 2, 8, 2.0)),
        "cotangent": scatter_about(arg_keys[1], (PAGES, SLOTS, D), 1.0, 6.0, ((0, 8), (1, 4))),
        "lengths": draw_lengths(jax.random.fold_in(arg_keys[18], 71), 0),
        "w_query": scatter_about(arg_keys[3], (D, D), D ** -0.5, 0.1875),
        "b_query": scatter_about(arg_keys[4], (D,), 0.3, 4.0, (), jnp.float32),
        "w_key": scatter_about(arg_keys[5], (D, D), D ** -0.5, 0.1875),
        "w_value": scatter_about(arg_keys[6], (D, D), D ** -0.5, 0.1875),
        "b_value": scatter_about(arg_keys[7], (D,), 0.3, 4.0, (), jnp.float32),
        "w_output": scatter_about(arg_keys[8], (D, D), (D // 16) ** -0.5, 0.75),
        "b_output": scatter_about(arg_keys[9], (D,), 0.3, 4.0, (), jnp.float32),
        "gain_first": jnp.clip(1.0 + 0.1 * jax.random.normal(arg_keys[10], (D,), jnp.float32), 0.5, 1.5),
        "shift_first": scatter_about(arg_keys[11], (D,), 0.3, 4.0, (), jnp.float32),
        "w_in": scatter_about(arg_keys[12], (D, FF), D ** -0.5, 0.1875),
        "b_in": scatter_about(arg_keys[13], (FF,), 0.3, 4.0, (), jnp.float32),
        "w_out": scatter_about(arg_keys[14], (FF, D), (FF // 4) ** -0.5, 0.1875),
        "b_out": scatter_about(arg_keys[15], (D,), 0.3, 4.0, (), jnp.float32),
        "gain_second": jnp.clip(1.0 + 0.1 * jax.random.normal(arg_keys[16], (D,), jnp.float32), 0.5, 1.5),
        "shift_second": scatter_about(arg_keys[17], (D,), 0.3, 4.0, (), jnp.float32),
    }


@jax.custom_vjp
def low(v):
    return lax.optimization_barrier(v.astype(jnp.bfloat16)).astype(jnp.float32)

@jax.custom_vjp
def low_back(v):
    return v

def low_keep(v):
    return (low(v), None)

def low_pass(kept, grad):
    return (grad,)

def back_keep(v):
    return (v, None)

def back_low(kept, grad):
    return (low(grad),)
low.defvjp(low_keep, low_pass)
low_back.defvjp(back_keep, back_low)
EPS = 1e-05
precise = lax.Precision.HIGHEST

def matmul_high(left, right):
    return jnp.matmul(left, right, precision=precise)

def layer_norm(summed, gain, shift):
    centred = summed - lax.optimization_barrier(jnp.mean(summed, -1, keepdims=True))
    normed = centred * lax.rsqrt(lax.optimization_barrier(jnp.mean(centred * centred, -1, keepdims=True)) + EPS)
    return normed * gain + shift

def attend_page(pieces):
    page_queries, page_keys, page_values, length = pieces
    page_queries = page_queries.reshape(SLOTS, HEADS, HEAD_DIM)
    page_keys = page_keys.reshape(SLOTS, HEADS, HEAD_DIM)
    page_values = page_values.reshape(SLOTS, HEADS, HEAD_DIM)
    scores = jnp.einsum('qhd,khd->hqk', page_queries, page_keys, precision=precise) * HEAD_DIM ** (-0.5)
    scores = low_back(scores)
    alive = jnp.arange(SLOTS) < length
    scores = jnp.where(alive[None, None, :], scores, -1e+30)
    weights = low(jax.nn.softmax(scores, axis=-1))
    context = jnp.einsum('hqk,khd->qhd', weights, page_values, precision=precise)
    return context.reshape(SLOTS, D)

def forward(inputs, lengths, w_query, b_query, w_key, w_value, b_value, w_output, b_output, gain_first, shift_first, w_in, b_in, w_out, b_out, gain_second, shift_second):
    queries = low_back(low(matmul_high(inputs, w_query) + b_query))
    keys_all = low_back(low(matmul_high(inputs, w_key)))
    values = low_back(low(matmul_high(inputs, w_value) + b_value))
    context = lax.map(jax.checkpoint(attend_page), (queries, keys_all, values, lengths))
    context = low_back(low(context))
    attended = low_back(matmul_high(context, w_output) + b_output)
    hidden = layer_norm(inputs + attended, gain_first, shift_first)
    inner = low_back(matmul_high(low(hidden), w_in) + b_in)
    activated = low(jax.nn.gelu(inner, approximate=False))
    branch = low_back(matmul_high(activated, w_out) + b_out)
    return layer_norm(hidden + branch, gain_second, shift_second)

def reference(inputs, cotangent, lengths, w_query, b_query, w_key, w_value, b_value, w_output, b_output, gain_first, shift_first, w_in, b_in, w_out, b_out, gain_second, shift_second):
    params = [weight.astype(jnp.float32) for weight in (w_query, b_query, w_key, w_value, b_value, w_output, b_output, gain_first, shift_first, w_in, b_in, w_out, b_out, gain_second, shift_second)]
    groups = PAGES // P_DEV

    def one_group(totals, pieces):
        block, upstream, block_lengths = pieces

        def apply(block_f32, *arrays):
            return forward(block_f32, block_lengths, *arrays)
        result, pull = jax.vjp(apply, block.astype(jnp.float32), *params)
        alive = (jnp.arange(SLOTS)[None, :] < block_lengths[:, None]).astype(jnp.float32)
        grads = pull(upstream.astype(jnp.float32) * alive[:, :, None])
        totals = tuple((total + grad for total, grad in zip(totals, grads[1:])))
        return (totals, (result.astype(jnp.bfloat16), grads[0]))
    start = tuple((jnp.zeros(weight.shape, jnp.float32) for weight in params))
    totals, (results, input_grads) = lax.scan(one_group, start, (inputs.reshape(groups, P_DEV, SLOTS, D), cotangent.reshape(groups, P_DEV, SLOTS, D), lengths.reshape(groups, P_DEV)))
    return (results.reshape(PAGES, SLOTS, D), input_grads.reshape(PAGES, SLOTS, D), totals[0], totals[1], totals[2], totals[3], totals[4], totals[5], totals[6], totals[7], totals[8], totals[9], totals[10], totals[11], totals[12], totals[13], totals[14])
```

```python
import math

import jax
import jax.numpy as jnp
from jax import lax
from jax.sharding import PartitionSpec as P

HEAD_DIM = 64
EPS = 1e-05


def dense(left, right):
    return jnp.dot(left, right, preferred_element_type=jnp.float32)


def dense_back(left, right):
    return lax.dot_general(
        left, right, (((1,), (1,)), ((), ())), preferred_element_type=jnp.float32
    )


def weight_term(left, right):
    return lax.dot_general(
        left, right, (((0,), (0,)), ((), ())), preferred_element_type=jnp.float32
    )


def norm_parts(summed):
    centred = summed - jnp.mean(summed, -1, keepdims=True)
    factor = lax.rsqrt(jnp.mean(centred * centred, -1, keepdims=True) + EPS)
    return (centred * factor, factor)


def norm_back(grad_normed, normed, factor):
    return factor * (
        grad_normed
        - jnp.mean(grad_normed, -1, keepdims=True)
        - normed * jnp.mean(grad_normed * normed, -1, keepdims=True)
    )


def stay(values):
    return values.astype(jnp.bfloat16)


def swap_stage(piece, axis, bit):
    count = lax.axis_size("dp")
    mine = (lax.axis_index("dp") >> bit) & 1
    keep = lax.dynamic_index_in_dim(piece, mine, axis, keepdims=False)
    send = lax.dynamic_index_in_dim(piece, 1 - mine, axis, keepdims=False)
    got = lax.ppermute(send, "dp", [(src, src ^ (1 << bit)) for src in range(count)])
    return stay(keep.astype(jnp.float32) + got.astype(jnp.float32))


def line_sum(piece):
    count = lax.axis_size("seq")
    place = lax.axis_index("seq")

    def part(index):
        index = jnp.clip(index, 0, count - 1)
        return lax.dynamic_index_in_dim(piece, index, 0, keepdims=False)

    right = left = None
    for step in range(1, count):
        up = part(count - step + place)
        down = part(place + step - count)
        if right is not None:
            up = stay(up.astype(jnp.float32) + right.astype(jnp.float32))
            down = stay(down.astype(jnp.float32) + left.astype(jnp.float32))
        right = lax.ppermute(up, "seq", [(z, z + 1) for z in range(min(step, count - 1))])
        left = lax.ppermute(
            down, "seq", [(count - 1 - z, count - 2 - z) for z in range(min(step, count - 1))]
        )
    own = part(place).astype(jnp.float32)
    if right is None:
        return own
    return own + right.astype(jnp.float32) + left.astype(jnp.float32)


def scatter_sum(term):
    dp = lax.axis_size("dp")
    seq = lax.axis_size("seq")
    bits = dp.bit_length() - 1
    rows, columns = term.shape
    depth = rows // (dp * seq)
    if dp != 1 << bits:
        return lax.psum_scatter(
            term.astype(jnp.float32), ("dp", "seq"), scatter_dimension=0, tiled=True
        )
    piece = term.reshape((2,) * bits + (seq, depth, columns))
    piece = swap_stage(piece, bits - 1, 0)
    halves = []
    others = list(range(1, bits))
    for part in range(2):
        half = piece[..., part * (columns // 2) : (part + 1) * (columns // 2)]
        order = others if part == 0 else others[::-1]
        left = sorted(others, reverse=True)
        for bit in order:
            half = swap_stage(half, left.index(bit), bit)
            left.remove(bit)
        halves.append(line_sum(half))
    return jnp.concatenate(halves, -1)


def small_sum(vectors):
    shards = lax.axis_size("dp") * lax.axis_size("seq")
    joined = jnp.concatenate([vector.reshape(shards, -1) for vector in vectors], 1)
    summed = lax.psum_scatter(joined, ("dp", "seq"), scatter_dimension=0, tiled=True)[0]
    out = []
    start = 0
    for vector in vectors:
        width = vector.shape[0] // shards
        out.append(summed[start : start + width])
        start += width
    return out


def to_pages(block):
    return lax.all_to_all(block, "seq", split_axis=0, concat_axis=1, tiled=True)


def to_slots(block):
    return lax.all_to_all(block, "seq", split_axis=1, concat_axis=0, tiled=True)


def on_device(
    inputs,
    cotangent,
    lengths,
    w_query,
    b_query,
    w_key,
    w_value,
    b_value,
    w_output,
    b_output,
    gain_first,
    shift_first,
    w_in,
    b_in,
    w_out,
    b_out,
    gain_second,
    shift_second,
):
    block = to_pages(inputs)
    upstream = to_pages(cotangent)
    pages, slots, width = block.shape
    rows = pages * slots
    heads = width // HEAD_DIM
    scale = 1.0 / math.sqrt(HEAD_DIM)
    page_lengths = lax.dynamic_slice_in_dim(lengths, lax.axis_index("seq") * pages, pages)
    live = jnp.arange(slots, dtype=jnp.int32)[None, :] < page_lengths[:, None]
    row_live = live.reshape(rows, 1).astype(jnp.float32)
    block = block.reshape(rows, width)
    upstream = upstream.reshape(rows, width).astype(jnp.float32) * row_live

    def by_head(array):
        return array.reshape(pages, slots, heads, HEAD_DIM)

    queries = (dense(block, w_query) + b_query).astype(jnp.bfloat16)
    keys = dense(block, w_key).astype(jnp.bfloat16)
    values = (dense(block, w_value) + b_value).astype(jnp.bfloat16)
    head_q, head_k, head_v = by_head(queries), by_head(keys), by_head(values)
    scores = (
        jnp.einsum("gqhd,gkhd->ghqk", head_q, head_k, preferred_element_type=jnp.float32) * scale
    )
    scores = jnp.where(live[:, None, None, :], scores, -1e30)
    largest = jnp.max(scores, -1, keepdims=True)
    expon = jnp.exp(scores - largest)
    probs = expon / jnp.sum(expon, -1, keepdims=True)
    probs_low = probs.astype(jnp.bfloat16)
    context = jnp.einsum("ghqk,gkhd->gqhd", probs_low, head_v, preferred_element_type=jnp.float32)
    context = context.astype(jnp.bfloat16).reshape(rows, width)
    attended = dense(context, w_output) + b_output
    normed_first, factor_first = norm_parts(block.astype(jnp.float32) + attended)
    hidden = normed_first * gain_first + shift_first
    hidden_low = hidden.astype(jnp.bfloat16)
    inner = dense(hidden_low, w_in) + b_in
    cumulative = 0.5 * (1.0 + lax.erf(inner * 0.7071067811865476))
    activated = (inner * cumulative).astype(jnp.bfloat16)
    slope = cumulative + inner * (jnp.exp(-0.5 * inner * inner) * 0.3989422804014327)
    branch = dense(activated, w_out) + b_out
    normed_second, factor_second = norm_parts(hidden + branch)
    result = (normed_second * gain_second + shift_second).astype(jnp.bfloat16)
    result = to_slots(result.reshape(pages, slots, width))

    g_gain_second = jnp.sum(upstream * normed_second, 0)
    g_shift_second = jnp.sum(upstream, 0)
    d_second = norm_back(upstream * gain_second, normed_second, factor_second)
    d_branch = d_second.astype(jnp.bfloat16)
    g_w_out = scatter_sum(stay(weight_term(activated, d_branch)))
    g_b_out = jnp.sum(d_branch.astype(jnp.float32), 0)
    d_inner = (dense_back(d_branch, w_out) * slope).astype(jnp.bfloat16)
    g_w_in = scatter_sum(stay(weight_term(hidden_low, d_inner)))
    g_b_in = jnp.sum(d_inner.astype(jnp.float32), 0)
    d_hidden = d_second + dense_back(d_inner, w_in)
    g_gain_first = jnp.sum(d_hidden * normed_first, 0)
    g_shift_first = jnp.sum(d_hidden, 0)
    d_first = norm_back(d_hidden * gain_first, normed_first, factor_first)
    d_attended = d_first.astype(jnp.bfloat16)
    g_w_output = scatter_sum(stay(weight_term(context, d_attended)))
    g_b_output = jnp.sum(d_attended.astype(jnp.float32), 0)
    head_grad = by_head(dense_back(d_attended, w_output).astype(jnp.bfloat16))
    d_probs = jnp.einsum("gqhd,gkhd->ghqk", head_grad, head_v, preferred_element_type=jnp.float32)
    d_vals = jnp.einsum("ghqk,gqhd->gkhd", probs_low, head_grad, preferred_element_type=jnp.float32)
    inner_sum = jnp.sum(probs * d_probs, -1, keepdims=True)
    d_scores = (probs * (d_probs - inner_sum)).astype(jnp.bfloat16)
    d_queries = (
        jnp.einsum("ghqk,gkhd->gqhd", d_scores, head_k, preferred_element_type=jnp.float32) * scale
    )
    d_keys = (
        jnp.einsum("ghqk,gqhd->gkhd", d_scores, head_q, preferred_element_type=jnp.float32) * scale
    )
    d_queries = d_queries.astype(jnp.bfloat16).reshape(rows, width)
    d_keys = d_keys.astype(jnp.bfloat16).reshape(rows, width)
    d_vals = d_vals.astype(jnp.bfloat16).reshape(rows, width)
    g_w_query = scatter_sum(stay(weight_term(block, d_queries)))
    g_w_key = scatter_sum(stay(weight_term(block, d_keys)))
    g_w_value = scatter_sum(stay(weight_term(block, d_vals)))
    g_b_query = jnp.sum(d_queries.astype(jnp.float32), 0)
    g_b_value = jnp.sum(d_vals.astype(jnp.float32), 0)
    grad_block = (
        d_first
        + dense_back(d_queries, w_query)
        + dense_back(d_keys, w_key)
        + dense_back(d_vals, w_value)
    )
    grad_block = to_slots(grad_block.astype(jnp.bfloat16).reshape(pages, slots, width))
    small = small_sum(
        [
            g_b_query,
            g_b_value,
            g_b_output,
            g_gain_first,
            g_shift_first,
            g_b_in,
            g_b_out,
            g_gain_second,
            g_shift_second,
        ]
    )
    return (
        result,
        grad_block.astype(jnp.float32),
        g_w_query,
        small[0],
        g_w_key,
        g_w_value,
        small[1],
        g_w_output,
        small[2],
        small[3],
        small[4],
        g_w_in,
        small[5],
        g_w_out,
        small[6],
        small[7],
        small[8],
    )


def solution(mesh):
    in_specs = (
        P("dp", "seq", None),
        P("dp", "seq", None),
        P("dp"),
        P(),
        P(),
        P(),
        P(),
        P(),
        P(),
        P(),
        P(),
        P(),
        P(),
        P(),
        P(),
        P(),
        P(),
        P(),
    )
    out_specs = (
        P("dp", "seq", None),
        P("dp", "seq", None),
        P(("dp", "seq"), None),
        P(("dp", "seq")),
        P(("dp", "seq"), None),
        P(("dp", "seq"), None),
        P(("dp", "seq")),
        P(("dp", "seq"), None),
        P(("dp", "seq")),
        P(("dp", "seq")),
        P(("dp", "seq")),
        P(("dp", "seq"), None),
        P(("dp", "seq")),
        P(("dp", "seq"), None),
        P(("dp", "seq")),
        P(("dp", "seq")),
        P(("dp", "seq")),
    )
    return jax.shard_map(
        on_device, mesh=mesh, in_specs=in_specs, out_specs=out_specs, check_vma=False
    )
```

```python
import math

import jax
import jax.numpy as jnp
from jax import lax
from jax.sharding import PartitionSpec as P

HEAD_DIM = 64
EPS = 1e-05


def dense(left, right):
    return jnp.dot(left, right, preferred_element_type=jnp.float32)


def dense_back(left, right):
    return lax.dot_general(
        left, right, (((1,), (1,)), ((), ())), preferred_element_type=jnp.float32
    )


def weight_term(left, right):
    return lax.dot_general(
        left, right, (((0,), (0,)), ((), ())), preferred_element_type=jnp.float32
    )


def norm_parts(summed):
    centred = summed - jnp.mean(summed, -1, keepdims=True)
    factor = lax.rsqrt(jnp.mean(centred * centred, -1, keepdims=True) + EPS)
    return (centred * factor, factor)


def norm_back(grad_normed, normed, factor):
    return factor * (
        grad_normed
        - jnp.mean(grad_normed, -1, keepdims=True)
        - normed * jnp.mean(grad_normed * normed, -1, keepdims=True)
    )


def stay(values):
    return values.astype(jnp.bfloat16)


def tie(*values):
    return lax.optimization_barrier(values)


def swap_bit(pieces, axis, bit):
    count = lax.axis_size("dp")
    mine = (lax.axis_index("dp") >> bit) & 1

    def side(which):
        parts = [lax.dynamic_index_in_dim(piece, which, axis, keepdims=False) for piece in pieces]
        return parts[0] if len(parts) == 1 else jnp.concatenate(parts, -1)

    got = lax.ppermute(side(1 - mine), "dp", [(src, src ^ (1 << bit)) for src in range(count)])
    return stay(side(mine).astype(jnp.float32) + got.astype(jnp.float32))


def open_sum(terms):
    dp = lax.axis_size("dp")
    seq = lax.axis_size("seq")
    bits = dp.bit_length() - 1
    pieces = []
    for term in terms:
        rows, columns = term.shape
        pieces.append(term.reshape((2,) * bits + (seq, rows // (dp * seq), columns)))
    piece = swap_bit(pieces, bits - 1, 0)
    cut = piece.shape[-1] // 256 * 128
    left = list(range(bits - 1, 0, -1))
    return [(piece[..., :cut], left, left[::-1]), (piece[..., cut:], left, left)]


def next_sum(halves):
    out = []
    for half, left, order in halves:
        bit = order[0]
        half = swap_bit([half], left.index(bit), bit)
        out.append((half, [other for other in left if other != bit], order[1:]))
    return out


def spread_sum(halves):
    while halves[0][2]:
        halves = next_sum(halves)
    piece = jnp.concatenate([half for half, _, _ in halves], -1)
    return lax.all_to_all(piece, "seq", split_axis=0, concat_axis=0, tiled=True)


def close_sum(spread):
    return jnp.sum(spread.astype(jnp.float32), 0)


def held(halves, *values):
    done = tie(*[half for half, _, _ in halves], *values)
    count = len(halves)
    halves = [(done[i], halves[i][1], halves[i][2]) for i in range(count)]
    return (halves, *done[count:])


def row_sum(array):
    ones = jnp.ones((8, array.shape[0]), jnp.bfloat16)
    return dense(ones, array)[0]


def lay_small(vectors, depth):
    shards = lax.axis_size("dp") * lax.axis_size("seq")
    joined = jnp.concatenate([vector.reshape(shards, -1) for vector in vectors], 1)
    width = joined.shape[1]
    joined = jnp.pad(joined, ((0, 0), (0, depth * 128 - width)))
    return stay(joined).reshape(shards * depth, 128)


def take_small(summed, sizes):
    flat = summed.reshape(-1)
    shards = lax.axis_size("dp") * lax.axis_size("seq")
    out = []
    start = 0
    for size in sizes:
        out.append(flat[start : start + size // shards])
        start += size // shards
    return out


def to_pages(block):
    count = lax.axis_size("seq")
    pages_dev, slots_dev, width = block.shape
    pages = pages_dev // count
    spread = lax.all_to_all(
        block.reshape(count, pages, slots_dev, width), "seq", split_axis=0, concat_axis=0, tiled=True
    )
    return spread.swapaxes(0, 1).reshape(pages, count * slots_dev, width)


def to_slots(block):
    count = lax.axis_size("seq")
    pages, slots, width = block.shape
    split = block.reshape(pages, count, slots // count, width).swapaxes(0, 1)
    spread = lax.all_to_all(split, "seq", split_axis=0, concat_axis=0, tiled=True)
    return spread.reshape(count * pages, slots // count, width)


def on_device(
    inputs,
    cotangent,
    lengths,
    w_query,
    b_query,
    w_key,
    w_value,
    b_value,
    w_output,
    b_output,
    gain_first,
    shift_first,
    w_in,
    b_in,
    w_out,
    b_out,
    gain_second,
    shift_second,
):
    block = to_pages(inputs)
    pages, slots, width = block.shape
    rows = pages * slots
    heads = width // HEAD_DIM
    scale = 1.0 / math.sqrt(HEAD_DIM)
    page_lengths = lax.dynamic_slice_in_dim(lengths, lax.axis_index("seq") * pages, pages)
    live = jnp.arange(slots, dtype=jnp.int32)[None, :] < page_lengths[:, None]
    row_live = live.reshape(rows, 1).astype(jnp.float32)
    block = block.reshape(rows, width)

    def by_head(array):
        return array.reshape(pages, slots, heads, HEAD_DIM)

    queries = (dense(block, w_query) + b_query).astype(jnp.bfloat16)
    queries, cotangent = tie(queries, cotangent)
    upstream = to_pages(cotangent)
    upstream = upstream.reshape(rows, width).astype(jnp.float32) * row_live
    keys = dense(block, w_key).astype(jnp.bfloat16)
    values = (dense(block, w_value) + b_value).astype(jnp.bfloat16)
    head_q, head_k, head_v = by_head(queries), by_head(keys), by_head(values)
    scores = (
        jnp.einsum("gqhd,gkhd->ghqk", head_q, head_k, preferred_element_type=jnp.float32) * scale
    )
    scores = jnp.where(live[:, None, None, :], scores, -1e30)
    largest = jnp.max(scores, -1, keepdims=True)
    expon = jnp.exp(scores - largest)
    probs = expon / jnp.sum(expon, -1, keepdims=True)
    probs_low = probs.astype(jnp.bfloat16)
    context = jnp.einsum("ghqk,gkhd->gqhd", probs_low, head_v, preferred_element_type=jnp.float32)
    context = context.astype(jnp.bfloat16).reshape(rows, width)
    attended = dense(context, w_output) + b_output
    normed_first, factor_first = norm_parts(block.astype(jnp.float32) + attended)
    hidden = normed_first * gain_first + shift_first
    hidden_low = hidden.astype(jnp.bfloat16)
    inner = dense(hidden_low, w_in) + b_in
    cumulative = 0.5 * (1.0 + lax.erf(inner * 0.7071067811865476))
    activated = (inner * cumulative).astype(jnp.bfloat16)
    slope = cumulative + inner * (jnp.exp(-0.5 * inner * inner) * 0.3989422804014327)
    branch = dense(activated, w_out) + b_out
    normed_second, factor_second = norm_parts(hidden + branch)
    result = (normed_second * gain_second + shift_second).astype(jnp.bfloat16)
    result = to_slots(result.reshape(pages, slots, width))

    g_gain_second = row_sum(stay(upstream * normed_second))
    g_shift_second = row_sum(stay(upstream))
    d_second = norm_back(upstream * gain_second, normed_second, factor_second)
    d_branch = d_second.astype(jnp.bfloat16)
    sum_out = open_sum([stay(weight_term(activated, d_branch))])
    d_inner = (dense_back(d_branch, w_out) * slope).astype(jnp.bfloat16)
    sum_out, d_inner = held(sum_out, d_inner)
    sum_out = next_sum(sum_out)
    sum_in = open_sum([stay(weight_term(hidden_low, d_inner))])
    g_b_out = row_sum(d_branch)
    g_b_in = row_sum(d_inner)
    d_hidden = d_second + dense_back(d_inner, w_in)
    g_gain_first = row_sum(stay(d_hidden * normed_first))
    g_shift_first = row_sum(stay(d_hidden))
    d_first = norm_back(d_hidden * gain_first, normed_first, factor_first)
    d_attended = d_first.astype(jnp.bfloat16)
    g_b_output = row_sum(d_attended)
    head_grad = dense_back(d_attended, w_output).astype(jnp.bfloat16)
    sum_out, head_grad = held(sum_out, head_grad)
    sum_in, head_grad = held(sum_in, head_grad)
    sum_out = next_sum(sum_out)
    d_vals = jnp.einsum(
        "ghqk,gqhd->gkhd", probs_low, by_head(head_grad), preferred_element_type=jnp.float32
    )
    d_vals = d_vals.astype(jnp.bfloat16).reshape(rows, width)
    sum_out, head_grad, d_vals = held(sum_out, head_grad, d_vals)
    spread_out = spread_sum(sum_out)
    sum_in = next_sum(sum_in)
    d_probs = jnp.einsum(
        "gqhd,gkhd->ghqk", by_head(head_grad), head_v, preferred_element_type=jnp.float32
    )
    inner_sum = jnp.sum(probs * d_probs, -1, keepdims=True)
    d_scores = (probs * (d_probs - inner_sum)).astype(jnp.bfloat16)
    sum_in, d_scores = held(sum_in, d_scores)
    sum_in = next_sum(sum_in)
    d_queries = (
        jnp.einsum("ghqk,gkhd->gqhd", d_scores, head_k, preferred_element_type=jnp.float32) * scale
    )
    d_keys = (
        jnp.einsum("ghqk,gqhd->gkhd", d_scores, head_q, preferred_element_type=jnp.float32) * scale
    )
    d_queries = d_queries.astype(jnp.bfloat16).reshape(rows, width)
    d_keys = d_keys.astype(jnp.bfloat16).reshape(rows, width)
    sum_in, d_queries, d_keys, spread_out = held(sum_in, d_queries, d_keys, spread_out)
    spread_in = spread_sum(sum_in)
    g_b_query = row_sum(d_queries)
    g_b_value = row_sum(d_vals)
    g_w_output = stay(weight_term(context, d_attended))
    g_w_query = stay(weight_term(block, d_queries))
    g_w_key = stay(weight_term(block, d_keys))
    g_w_value = stay(weight_term(block, d_vals))
    vectors = [
        g_b_query,
        g_b_value,
        g_b_output,
        g_gain_first,
        g_shift_first,
        g_b_in,
        g_b_out,
        g_gain_second,
        g_shift_second,
    ]
    shards = lax.axis_size("dp") * lax.axis_size("seq")
    small = lay_small(vectors, width // shards)
    sum_low = open_sum([g_w_query, g_w_key, g_w_value, g_w_output, small])
    grad_block = (
        d_first
        + dense_back(d_queries, w_query)
        + dense_back(d_keys, w_key)
        + dense_back(d_vals, w_value)
    )
    grad_block = to_slots(grad_block.astype(jnp.bfloat16).reshape(pages, slots, width))
    g_w_out = close_sum(spread_out)
    g_w_in = close_sum(spread_in)
    low = close_sum(spread_sum(sum_low))
    small = take_small(low[:, 4 * width :], [vector.shape[0] for vector in vectors])
    return (
        result,
        grad_block.astype(jnp.float32),
        low[:, :width],
        small[0],
        low[:, width : 2 * width],
        low[:, 2 * width : 3 * width],
        small[1],
        low[:, 3 * width : 4 * width],
        small[2],
        small[3],
        small[4],
        g_w_in,
        small[5],
        g_w_out,
        small[6],
        small[7],
        small[8],
    )


def solution(mesh):
    in_specs = (
        P("dp", "seq", None),
        P("dp", "seq", None),
        P("dp"),
        P(),
        P(),
        P(),
        P(),
        P(),
        P(),
        P(),
        P(),
        P(),
        P(),
        P(),
        P(),
        P(),
        P(),
        P(),
    )
    out_specs = (
        P("dp", "seq", None),
        P("dp", "seq", None),
        P(("dp", "seq"), None),
        P(("dp", "seq")),
        P(("dp", "seq"), None),
        P(("dp", "seq"), None),
        P(("dp", "seq")),
        P(("dp", "seq"), None),
        P(("dp", "seq")),
        P(("dp", "seq")),
        P(("dp", "seq")),
        P(("dp", "seq"), None),
        P(("dp", "seq")),
        P(("dp", "seq"), None),
        P(("dp", "seq")),
        P(("dp", "seq")),
        P(("dp", "seq")),
    )
    return jax.shard_map(
        on_device, mesh=mesh, in_specs=in_specs, out_specs=out_specs, check_vma=False
    )
```
